32 devices in a mesh: dp: 4 (over y, x), proto: 4 (over z), pair: 2 (over core).
Axes of the slice: x: 2, y: 2, z: 4, core: 2. Of those that a mesh axis runs over, the one named last changes fastest.
Arguments:
- student_patches: bfloat16 [2, 4096, 256], P('pair', 'dp'), may hold values from -2 to 2
- teacher_patches: bfloat16 [2, 4096, 256], P('pair', 'dp'), may hold values from -8 to 8
- student_proto: bfloat16 [65536, 256], P('proto'), may hold values from -4 to 4
- teacher_proto: bfloat16 [65536, 256], P('proto'), may hold values from -4 to 4
- masked_rows: int32 [2, 1024], P('pair', 'dp'), may hold values from 0 to 1023, as said below
Outputs:
- student_grad: float32 [2, 1024, 256], P('pair', 'dp')
The draws below stay inside these ranges and needn't reach their ends.
Inputs may be any that keep to these rules, and one draw needn't show every extreme that they name: `masked_rows`: entries of one device's block name distinct patch rows of that device's 4 images (image g owns rows g * 256 to (g + 1) * 256 - 1); every image has between 16 and 112 masked patches.
All inputs are finite; a program needn't handle non-finite values.
Results may differ from the reference program's by a relative error of at most 0.00075.
The reference program's roundings to bfloat16 on the way (of `targets` and `pushed_w`) count: a program that leaves them out, or rounds other values in their place, can miss the bound.
Values sent between devices are 32-bit elements; how exact they have to be, the bound alone decides.
No kernel may reach another device: no remote copies, remote signals or barrier semaphores. Data moves between devices by JAX's collectives and lax.ppermute only.
A program may use at most 128 MiB of HBM per device.

```python
import math
import jax
import jax.numpy as jnp
from jax import lax

D = 256
K = 65536
PATCHES = 256
ITERS = 2
IMG_DEV = 4
MASK_DEV = 256
IMAGES = 16
MASKED = 1024
N_DP = 4


def noise_table(key, shape):
    return jnp.clip(jax.random.normal(key, shape, jnp.float32), -6.0, 6.0)


def log_spread(key, shape, lower, upper):
    return jnp.exp(jax.random.uniform(key, shape, jnp.float32, math.log(lower), math.log(upper)))


def teacher_table(key):
    base_key = jax.random.fold_in(key, 7)
    noise_key = jax.random.fold_in(base_key, 1)
    scale_key = jax.random.fold_in(base_key, 2)
    return (noise_table(noise_key, (K, D)), log_spread(scale_key, (K, 1), 1.0, 10.0))


def draw_teacher_proto(key, part):
    base, scales = teacher_table(key)
    return jnp.clip(base * scales / 16.0, -4.0, 4.0).astype(jnp.bfloat16)


def draw_teacher_patches(key, part):
    base, scales = teacher_table(key)
    total = IMAGES * PATCHES
    chosen = jax.random.randint(jax.random.fold_in(key, 21), (2, total), 0, K)
    picked = base[chosen]
    position = jnp.arange(total, dtype=jnp.float32) / total
    mixing = log_spread(jax.random.fold_in(key, 22), (2, total, 1), 0.7, 1.4) * (0.5 + 1.5 * position)[None, :, None]
    noise = noise_table(jax.random.fold_in(key, 23), (2, total, D))
    row_scale = log_spread(jax.random.fold_in(key, 24), (2, total, 1), 1.0, 10.0)
    values = (mixing * picked + noise) * row_scale / 16.0
    return jnp.clip(values, -8.0, 8.0).astype(jnp.bfloat16)


def draw_student_patches(key, part):
    total = IMAGES * PATCHES
    noise = noise_table(jax.random.fold_in(key, 41), (2, total, D))
    row_scale = log_spread(jax.random.fold_in(key, 42), (2, total, 1), 1.0, 10.0)
    values = noise * row_scale / 32.0
    return jnp.clip(values, -2.0, 2.0).astype(jnp.bfloat16)


def draw_student_proto(key, part):
    noise = noise_table(jax.random.fold_in(key, 51), (K, D))
    row_scale = log_spread(jax.random.fold_in(key, 52), (K, 1), 1.0, 10.0)
    return jnp.clip(noise * row_scale / 16.0, -4.0, 4.0).astype(jnp.bfloat16)


def shuffle(seed_key):
    return jax.random.permutation(seed_key, PATCHES).astype(jnp.int32)


def draw_masked_rows(key, part):
    half_patches = PATCHES // 2
    pair_total = IMAGES
    first_count = jax.random.randint(jax.random.fold_in(key, 31), (pair_total,), PATCHES // 16, 7 * PATCHES // 16 + 1)
    first_keys = jax.random.split(jax.random.fold_in(key, 32), pair_total)
    second_keys = jax.random.split(jax.random.fold_in(key, 33), pair_total)
    order_first = jax.vmap(shuffle)(first_keys)
    order_second = jax.vmap(shuffle)(second_keys)
    slot_index = jnp.arange(half_patches, dtype=jnp.int32)
    in_first = slot_index[None, :] < first_count[:, None]
    later = jnp.clip(slot_index[None, :] - first_count[:, None], 0, PATCHES - 1)
    patch = jnp.where(in_first, order_first[:, :half_patches], jnp.take_along_axis(order_second, later, axis=1))
    image = jnp.where(in_first, 0, 1)
    local_pair = jnp.arange(pair_total, dtype=jnp.int32) % (IMG_DEV // 2)
    rows = (2 * local_pair[:, None] + image) * PATCHES + patch
    return rows.reshape(2, MASKED).astype(jnp.int32)


def setup_inputs(seed: int = 0) -> dict:
    streams_of = jax.random.split(jax.random.key(seed), 6)
    return {
        "student_patches": draw_student_patches(jax.random.fold_in(streams_of[5], 71), 0),
        "teacher_patches": draw_teacher_patches(jax.random.fold_in(streams_of[5], 71), 0),
        "student_proto": draw_student_proto(jax.random.fold_in(streams_of[5], 71), 0),
        "teacher_proto": draw_teacher_proto(jax.random.fold_in(streams_of[5], 71), 0),
        "masked_rows": draw_masked_rows(jax.random.fold_in(streams_of[5], 71), 0),
    }


teacher_temp = 0.07
student_temp = 0.1
epsilon = 1e-06

def inverse_norms(matrix):
    return lax.rsqrt(lax.optimization_barrier(jnp.sum(jnp.square(matrix.astype(jnp.float32)), axis=-1)) + epsilon)

def reference(student_patches, teacher_patches, student_proto, teacher_proto, masked_rows):
    slot_index = jnp.arange(MASKED, dtype=jnp.int32)
    device_block = slot_index // MASK_DEV
    slot_rows = (device_block[None, :] * (IMG_DEV * PATCHES) + masked_rows).astype(jnp.int32)
    crop_index = jnp.arange(2, dtype=jnp.int32)[:, None]
    image_key = (device_block[None, :] * IMG_DEV + masked_rows // PATCHES).astype(jnp.int32)
    member = (image_key[:, :, None] == jnp.arange(IMAGES, dtype=jnp.int32)[None, None, :]).astype(jnp.float32)
    per_image = lax.optimization_barrier(jnp.sum(member, axis=1))
    slot_count = jnp.take_along_axis(per_image, image_key, axis=1)
    mask_weight = MASK_DEV / IMG_DEV / slot_count
    student_rows = student_patches[crop_index, slot_rows]
    teacher_rows = teacher_patches[crop_index, slot_rows]
    teacher_scale = inverse_norms(teacher_proto)
    student_scale = inverse_norms(student_proto)
    teacher_blocks = teacher_rows.reshape(2 * MASKED // MASK_DEV, MASK_DEV, D)

    def teacher_block(block):
        scores = jnp.dot(block, teacher_proto.T, preferred_element_type=jnp.float32)
        return jnp.exp(scores * inverse_norms(block)[:, None] * teacher_scale[None, :] / teacher_temp)
    teacher_exp = lax.map(teacher_block, teacher_blocks).reshape(2 * MASKED, K)
    row_factor = jnp.ones((2 * MASKED,), jnp.float32)
    column_factor = jnp.ones((K,), jnp.float32)
    for sweep in range(ITERS):
        column_factor = 1.0 / jnp.dot(row_factor, teacher_exp, precision=lax.Precision.HIGHEST)
        row_factor = 1.0 / jnp.dot(teacher_exp, column_factor, precision=lax.Precision.HIGHEST)
    target_scale = column_factor * student_scale
    teacher_exp = teacher_exp.reshape(2, MASKED, K)
    row_factor = row_factor.reshape(2, MASKED)
    student_inv = inverse_norms(student_rows)

    def student_block(start):
        exp_block = lax.dynamic_slice_in_dim(teacher_exp, start, MASK_DEV, axis=1)
        factor_block = lax.dynamic_slice_in_dim(row_factor, start, MASK_DEV, axis=1)
        targets = (exp_block * factor_block[:, :, None] * target_scale[None, None, :]).astype(jnp.bfloat16)
        targets = targets.reshape(2 * MASK_DEV, K)
        rows_block = lax.dynamic_slice_in_dim(student_rows, start, MASK_DEV, axis=1).reshape(2 * MASK_DEV, D)
        inv_block = lax.dynamic_slice_in_dim(student_inv, start, MASK_DEV, axis=1).reshape(2 * MASK_DEV)
        weight_block = lax.dynamic_slice_in_dim(mask_weight, start, MASK_DEV, axis=1).reshape(2 * MASK_DEV)
        logits = jnp.dot(rows_block, student_proto.T, preferred_element_type=jnp.float32)
        student_exp = jnp.exp(logits * inv_block[:, None] * student_scale[None, :] / student_temp)
        partition = lax.optimization_barrier(jnp.sum(student_exp, axis=1))
        pushed_w = (student_exp * student_scale[None, :]).astype(jnp.bfloat16)
        pushed = jnp.dot(pushed_w, student_proto, preferred_element_type=jnp.float32)
        pulled = jnp.dot(targets, student_proto, preferred_element_type=jnp.float32)
        inner_grad = (pushed / partition[:, None] - pulled) / student_temp
        rows_float = rows_block.astype(jnp.float32)
        row_dot = lax.optimization_barrier(jnp.sum(rows_float * inner_grad, axis=1))
        cube = inv_block * inv_block * inv_block
        result_grad = weight_block[:, None] * (inv_block[:, None] * inner_grad - rows_float * (cube * row_dot)[:, None])
        return result_grad.reshape(2, MASK_DEV, D)
    starts = (jnp.arange(N_DP, dtype=jnp.int32) * MASK_DEV).astype(jnp.int32)
    blocks = lax.map(student_block, starts)
    return jnp.transpose(blocks, (1, 0, 2, 3)).reshape(2, MASKED, D)
```

```python
import functools

import jax
import jax.numpy as jnp
from jax import lax
from jax.experimental import pallas as pl
from jax.experimental.pallas import tpu as pltpu
from jax.sharding import PartitionSpec as P

PATCHES = 256
LANES = 128
TILE = 256

teacher_temp = 0.07
student_temp = 0.1
epsilon = 1e-06
log2e = 1.4426950408889634

NT = (((1,), (1,)), ((), ()))
F32 = jnp.float32
BF16 = jnp.bfloat16
VMEM = pltpu.VMEM


def eye(n):
    return lax.broadcasted_iota(jnp.int32, (n, n), 0) == lax.broadcasted_iota(jnp.int32, (n, n), 1)


def to_column(row):
    n = row.shape[1]
    return jnp.sum(jnp.where(eye(n), jnp.broadcast_to(row, (n, n)), 0.0), axis=1, keepdims=True)


def to_row(column):
    n = column.shape[0]
    return jnp.sum(jnp.where(eye(n), jnp.broadcast_to(column, (n, n)), 0.0), axis=0, keepdims=True)


def tree(refs):
    parts = [ref[...] for ref in refs]
    while len(parts) > 1:
        parts = [parts[i] + parts[i + 1] for i in range(0, len(parts), 2)]
    return parts[0]


def gather_rows(slots, patches):
    column = to_column(slots.astype(F32)).astype(jnp.int32)
    count = slots.shape[1]
    rows = patches.shape[0]
    onehot = lax.broadcasted_iota(jnp.int32, (count, rows), 1) == column
    onehot = jnp.where(onehot, 1.0, 0.0).astype(BF16)
    return jnp.dot(onehot, patches, preferred_element_type=F32).astype(BF16)


def row_inverse(rows):
    wide = rows.astype(F32)
    return lax.rsqrt(jnp.sum(wide * wide, axis=1, keepdims=True) + epsilon)


def tile_scale(protos):
    gram = lax.dot_general(protos, protos, NT, preferred_element_type=F32)
    mask = eye(LANES)
    parts = []
    for k in range(0, TILE, LANES):
        parts.append(jnp.sum(jnp.where(mask, gram[k : k + LANES, k : k + LANES], 0.0), axis=0, keepdims=True))
    return lax.rsqrt(jnp.concatenate(parts, axis=1) + epsilon)


def teacher_kernel(slots_ref, patches_ref, protos_ref, exp_ref, sums_ref, rows_ref, factor_ref):
    block = protos_ref.shape[0]
    step = pl.program_id(0)

    @pl.when(step == 0)
    def _():
        rows = gather_rows(slots_ref[...], patches_ref[...])
        rows_ref[...] = rows
        factor = row_inverse(rows) * (log2e / teacher_temp)
        factor_ref[...] = jnp.broadcast_to(factor, factor_ref.shape)

    rows = rows_ref[...]
    for t in range(block // TILE):
        protos = protos_ref[t * TILE : (t + 1) * TILE, :]
        scores = lax.dot_general(rows, protos, NT, preferred_element_type=F32)
        scale = tile_scale(protos)
        for h in range(TILE // LANES):
            lanes = slice(h * LANES, (h + 1) * LANES)
            value = jnp.exp2(scores[:, lanes] * factor_ref[...] * scale[:, lanes])
            exp_ref[:, pl.ds(pl.multiple_of(step * block + t * TILE + h * LANES, LANES), LANES)] = value
            sums_ref[pl.ds(t * (TILE // LANES) + h, 1), :] = jnp.sum(value, axis=0, keepdims=True)


def student_kernel(
    slots_ref, patches_ref, protos_ref, scale_ref, part_ref, pushed_ref, rows_out_ref, rows_ref, factor_ref, total_ref, w_ref
):
    block = protos_ref.shape[0]
    step = pl.program_id(0)

    @pl.when(step == 0)
    def _():
        rows = gather_rows(slots_ref[...], patches_ref[...])
        rows_ref[...] = rows
        rows_out_ref[...] = rows
        factor = row_inverse(rows) * (log2e / student_temp)
        factor_ref[...] = jnp.broadcast_to(factor, factor_ref.shape)
        total_ref[...] = jnp.zeros_like(total_ref)
        pushed_ref[...] = jnp.zeros_like(pushed_ref)

    rows = rows_ref[...]
    for t in range(block // TILE):
        protos = protos_ref[t * TILE : (t + 1) * TILE, :]
        scores = lax.dot_general(rows, protos, NT, preferred_element_type=F32)
        scale = tile_scale(protos)
        for h in range(TILE // LANES):
            lanes = slice(h * LANES, (h + 1) * LANES)
            value = jnp.exp2(scores[:, lanes] * factor_ref[...] * scale[:, lanes])
            total_ref[...] += value
            w_ref[:, t * TILE + h * LANES : t * TILE + (h + 1) * LANES] = (value * scale[:, lanes]).astype(BF16)
            scale_ref[pl.ds(t * (TILE // LANES) + h, 1), :] = scale[:, lanes]
    pushed_ref[...] += jnp.dot(w_ref[...], protos_ref[...], preferred_element_type=F32)

    @pl.when(step == pl.num_programs(0) - 1)
    def _():
        part_ref[...] = to_row(jnp.sum(total_ref[...], axis=1, keepdims=True))


def row_pass_kernel(count, *refs):
    exp_ref = refs[0]
    column_ref, out_ref, total_ref = refs[1 + count :]
    column_ref[...] = 1.0 / tree(refs[1 : 1 + count])
    total_ref[...] = jnp.zeros_like(total_ref)
    chunks = exp_ref.shape[1] // LANES
    group = 8

    def body(g, carry):
        acc = total_ref[...]
        for k in range(group):
            c = g * group + k
            lanes = pl.ds(pl.multiple_of(c * LANES, LANES), LANES)
            acc = acc + exp_ref[:, lanes] * column_ref[pl.ds(c, 1), :]
        total_ref[...] = acc
        return carry

    lax.fori_loop(0, chunks // group, body, 0)
    out_ref[...] = to_row(jnp.sum(total_ref[...], axis=1, keepdims=True))


def column_pass_kernel(count, *refs):
    exp_ref = refs[0]
    out_ref, factor_ref = refs[1 + count :]
    factor = to_column(1.0 / tree(refs[1 : 1 + count]))
    factor_ref[...] = jnp.broadcast_to(factor, factor_ref.shape)
    chunks = exp_ref.shape[1] // LANES
    group = 4

    def body(g, carry):
        for k in range(group):
            c = g * group + k
            lanes = pl.ds(pl.multiple_of(c * LANES, LANES), LANES)
            out_ref[pl.ds(c, 1), :] = jnp.sum(exp_ref[:, lanes] * factor_ref[...], axis=0, keepdims=True)
        return carry

    lax.fori_loop(0, chunks // group, body, 0)


def pull_kernel(count, *refs):
    exp_ref = refs[0]
    column_ref, scale_ref, protos_ref, out_ref, factor_ref, w_ref = refs[1 + count :]
    block = protos_ref.shape[0]
    step = pl.program_id(0)

    @pl.when(step == 0)
    def _():
        factor = to_column(1.0 / tree(refs[1 : 1 + count]))
        factor_ref[...] = jnp.broadcast_to(factor, factor_ref.shape)
        out_ref[...] = jnp.zeros_like(out_ref)

    for k in range(block // LANES):
        lanes = pl.ds(pl.multiple_of(step * block + k * LANES, LANES), LANES)
        scale = column_ref[k : k + 1, :] * scale_ref[k : k + 1, :]
        w_ref[:, k * LANES : (k + 1) * LANES] = (exp_ref[:, lanes] * factor_ref[...] * scale).astype(BF16)
    out_ref[...] += jnp.dot(w_ref[...], protos_ref[...], preferred_element_type=F32)


def final_kernel(images, counts, *refs):
    out_ref = refs[-1]
    slots_ref, rows_ref = refs[:2]
    at = 2
    groups = []
    for count in counts:
        groups.append(tree(refs[at : at + count]))
        at += count
    partition, pushed, pulled = groups
    rows = rows_ref[...]
    inv = row_inverse(rows)
    wide = rows.astype(F32)
    grad = (pushed / to_column(partition) - pulled) / student_temp
    row_dot = jnp.sum(wide * grad, axis=1, keepdims=True)
    slots = slots_ref[...]
    total = slots.shape[1]
    image = (slots // PATCHES).astype(F32)
    same = to_column(image) == jnp.broadcast_to(image, (total, total))
    slot_count = jnp.sum(jnp.where(same, 1.0, 0.0), axis=1, keepdims=True)
    weights = total / images / slot_count
    out_ref[...] = weights * (inv * grad - wide * (inv * inv * inv * row_dot))


def exchange(value, axis):
    size = lax.axis_size(axis)
    if size > 4:
        while size > 4:
            size //= 2
            value = value + lax.ppermute(value, axis, [(i, i ^ size) for i in range(lax.axis_size(axis))])
    members = range(lax.axis_size(axis))
    return [value] + [lax.ppermute(value, axis, [(i, i ^ k) for i in members]) for k in range(1, size)]


def column_exchange(value):
    value = value + lax.ppermute(value, "pair", [(0, 1), (1, 0)])
    return exchange(value, "dp")


def call(kernel, name, out_shape, scratch=(), grid=None, in_specs=None, out_specs=None, limit=None):
    keep = {}
    if grid is not None:
        keep["grid"] = grid
    if in_specs is not None:
        keep["in_specs"] = in_specs
    if out_specs is not None:
        keep["out_specs"] = out_specs
    return pl.pallas_call(
        kernel,
        out_shape=out_shape,
        scratch_shapes=scratch,
        compiler_params=pltpu.CompilerParams(vmem_limit_bytes=limit or (36 << 20)),
        name=name,
        **keep,
    )


def whole(shape=None):
    return pl.BlockSpec(memory_space=VMEM)


def on_device(student_patches, teacher_patches, student_proto, teacher_proto, masked_rows):
    slots = masked_rows
    count = slots.shape[1]
    images = student_patches.shape[1] // PATCHES
    columns, width = teacher_proto.shape
    block = min(2048, columns)
    steps = columns // block
    chunks = columns // LANES
    shape = jax.ShapeDtypeStruct
    col_shape = shape((chunks, LANES), F32)
    row_shape = shape((1, count), F32)
    grad_shape = shape((count, width), F32)
    exp_shape = VMEM((count, columns), F32)
    col_block = pl.BlockSpec((block // LANES, LANES), lambda i: (i, 0))
    proto_block = pl.BlockSpec((block, width), lambda i: (i, 0))
    broad = VMEM((count, LANES), F32)
    full = whole()
    mib = 1 << 20

    exp, sums = call(
        teacher_kernel,
        "teacher",
        (exp_shape, col_shape),
        grid=(steps,),
        in_specs=[full, full, proto_block],
        out_specs=(full, col_block),
        scratch=[VMEM((count, width), BF16), broad],
    )(slots, teacher_patches[0], teacher_proto)

    scale, part, pushed, rows = call(
        student_kernel,
        "student",
        (col_shape, row_shape, grad_shape, shape((count, width), BF16)),
        grid=(steps,),
        in_specs=[full, full, proto_block],
        out_specs=(col_block, full, full, full),
        scratch=[VMEM((count, width), BF16), broad, broad, VMEM((count, block), BF16)],
    )(slots, student_patches[0], student_proto)

    def row_pass(parts):
        kernel = functools.partial(row_pass_kernel, len(parts))
        return call(kernel, "row_pass", (col_shape, row_shape), scratch=[broad])(exp, *parts)

    def column_pass(parts):
        kernel = functools.partial(column_pass_kernel, len(parts))
        return call(kernel, "column_pass", col_shape, scratch=[broad])(exp, *parts)

    column, row_part = row_pass(column_exchange(sums))
    sums = column_pass(exchange(row_part, "proto"))
    column, row_part = row_pass(column_exchange(sums))
    row_parts = exchange(row_part, "proto")
    pulled = call(
        functools.partial(pull_kernel, len(row_parts)),
        "pull",
        grad_shape,
        grid=(steps,),
        in_specs=[full] * (1 + len(row_parts)) + [col_block, col_block, proto_block],
        out_specs=full,
        scratch=[broad, VMEM((count, block), BF16)],
    )(exp, *row_parts, column, scale, student_proto)

    groups = [exchange(part, "proto"), exchange(pushed, "proto"), exchange(pulled, "proto")]
    flat = [value for group in groups for value in group]
    kernel = functools.partial(final_kernel, images, [len(group) for group in groups])
    return call(kernel, "final", grad_shape)(slots, rows, *flat)[None]


def solution(mesh):
    placed = (
        P("pair", "dp", None),
        P("pair", "dp", None),
        P("proto", None),
        P("proto", None),
        P("pair", "dp"),
    )
    return jax.shard_map(
        on_device, mesh=mesh, in_specs=placed, out_specs=P("pair", "dp", None), check_vma=False
    )
```
